32 devices in a mesh: dp: 4 (over x, core), blk: 4 (over z), ulysses: 2 (over y).
Axes of the slice: x: 2, y: 2, z: 4, core: 2. Of those that a mesh axis runs over, the one named last changes fastest.
Arguments:
- tokens: bfloat16 [8192, 768], P(('dp', 'blk', 'ulysses')), may hold values from -6 to 6
- cotangent: bfloat16 [8192, 768], P(('dp', 'blk', 'ulysses')), may hold values from -6 to 6
- lengths: int32 [4], P('dp'), may hold values from 512 to 2048, as said below
- stretch_order: int32 [8], replicated, may hold values from 0 to 7, each once
- gain_attn: bfloat16 [768], P(('dp', 'blk', 'ulysses')), may hold values from 0.5 to 1.5
- w_query: bfloat16 [768, 768], P(('dp', 'blk', 'ulysses')), may hold values from -0.21875 to 0.21875
- w_key: bfloat16 [768, 768], P(('dp', 'blk', 'ulysses')), may hold values from -0.21875 to 0.21875
- w_value: bfloat16 [768, 768], P(('dp', 'blk', 'ulysses')), may hold values from -0.21875 to 0.21875
- w_out: bfloat16 [768, 768], P(('dp', 'blk', 'ulysses')), may hold values from -3 to 3
- gain_ffn: bfloat16 [768], P(('dp', 'blk', 'ulysses')), may hold values from 0.5 to 1.5
- w_gate: bfloat16 [768, 2048], P(('dp', 'blk', 'ulysses')), may hold values from -0.21875 to 0.21875
- w_up: bfloat16 [768, 2048], P(('dp', 'blk', 'ulysses')), may hold values from -0.21875 to 0.21875
- w_down: bfloat16 [768, 2048], P(('dp', 'blk', 'ulysses')), may hold values from -0.5 to 0.5
Outputs:
- output: float32 [8192, 768], P(('dp', 'blk', 'ulysses'))
- grad_input: float32 [8192, 768], P(('dp', 'blk', 'ulysses'))
- grad_gain_attn: float32 [768], P(('dp', 'blk', 'ulysses'))
- grad_w_query: float32 [768, 768], P(('dp', 'blk', 'ulysses'))
- grad_w_key: float32 [768, 768], P(('dp', 'blk', 'ulysses'))
- grad_w_value: float32 [768, 768], P(('dp', 'blk', 'ulysses'))
- grad_w_out: float32 [768, 768], P(('dp', 'blk', 'ulysses'))
- grad_gain_ffn: float32 [768], P(('dp', 'blk', 'ulysses'))
- grad_w_gate: float32 [768, 2048], P(('dp', 'blk', 'ulysses'))
- grad_w_up: float32 [768, 2048], P(('dp', 'blk', 'ulysses'))
- grad_w_down: float32 [768, 2048], P(('dp', 'blk', 'ulysses'))
The draws below stay inside these ranges and needn't reach their ends.
Inputs may be any that keep to these rules, and one draw needn't show every extreme that they name: `lengths`: one sequence has all 2048 slots live and another 2048 // 4 in every draw. Each stretch number once; storage block j of every sequence holds its positions stretch_order[j] * 256 onward.
All inputs are finite; a program needn't handle non-finite values.
Results may differ from the reference program's by a relative error of at most 0.017.
Values may be sent and summed in bfloat16 or wider, within the bound.
No kernel may reach another device: no remote copies, remote signals or barrier semaphores. Data moves between devices by JAX's collectives and lax.ppermute only.
A program may use at most 128 MiB of HBM per device.

```python
import math
import jax
import jax.numpy as jnp
from jax import lax

D = 768
HEADS = 12
HEAD_DIM = 64
FF = 2048
SEQ = 2048
SEQS = 4
TOKENS = 8192
STRETCHES = 8


def draw_lengths(key, part):
    first_key = jax.random.fold_in(key, 11)
    second_key = jax.random.fold_in(key, 12)
    drawn = jax.random.randint(first_key, (SEQS,), SEQ // 4, SEQ + 1, dtype=jnp.int32)
    order = jax.random.permutation(second_key, SEQS)
    drawn = drawn.at[order[0]].set(SEQ)
    drawn = drawn.at[order[1]].set(SEQ // 4)
    return drawn.astype(jnp.int32)


def spiked(result, stream_key, source, target, blocks, factor):
    owner, partner = [(jnp.arange(result.shape[dim]) // (result.shape[dim] // blocks)).reshape([-1 if axis == dim else 1 for axis in range(result.ndim)]) for dim in (source, target)]
    chosen = jax.random.permutation(stream_key, blocks)[partner]
    strong = (owner == chosen) | (owner == (partner + blocks // 2) % blocks)
    return jnp.where(strong, factor * result, result)


def block_scale(stream_key, shape, split, least, largest):
    gain, own = 1.0, jax.random.fold_in(stream_key, 6)
    for axis_at, shards_of in split:
        draws = jnp.exp(jax.random.uniform(jax.random.fold_in(own, axis_at), (shards_of,), jnp.float32, least / len(split), largest / len(split)))
        gain = gain * jnp.repeat(draws, shape[axis_at] // shards_of).reshape([-1 if axis == axis_at else 1 for axis in range(len(shape))])
    return gain


def normal_values(key, extent, scale, reach, pieces=(), kind=jnp.bfloat16):
    factor_of = block_scale(key, extent, pieces, -0.22, 0.18) if pieces else 1.0
    array = jax.random.normal(key, extent, jnp.float32) * scale * factor_of
    return jnp.minimum(jnp.maximum(array, -reach), reach).astype(kind)


def gaussian_with(stream_key, shape, deviation, bound, pieces, heavy, kind=jnp.bfloat16):
    values = deviation * jax.random.normal(stream_key, shape, jnp.float32)
    if pieces:
        values = values * block_scale(stream_key, shape, pieces, -0.22, 0.18)
    return jnp.clip(spiked(values, jax.random.fold_in(stream_key, 3), *heavy), -bound, bound).astype(kind)


def setup_inputs(seed: int = 0) -> dict:
    splits = jax.random.split(jax.random.key(seed), 14)
    return {
        "tokens": normal_values(splits[0], (TOKENS, D), 1.0, 6.0, ((0, 32),)),
        "cotangent": gaussian_with(splits[1], (TOKENS, D), 1.0, 6.0, ((0, 32),), (0, 1, 32, 2.75)),
        "lengths": draw_lengths(jax.random.fold_in(splits[13], 71), 0),
        "stretch_order": jax.random.permutation(splits[3], STRETCHES).astype(jnp.int32),
        "gain_attn": jnp.clip(1.0 + 0.1 * jax.random.normal(splits[4], (D,), jnp.float32), 0.5, 1.5).astype(jnp.bfloat16),
        "w_query": normal_values(splits[5], (D, D), D ** -0.5, 0.21875, ((0, 32),)),
        "w_key": normal_values(splits[6], (D, D), D ** -0.5, 0.21875, ((0, 32),)),
        "w_value": normal_values(splits[7], (D, D), D ** -0.5, 0.21875, ((0, 32),)),
        "w_out": normal_values(splits[8], (D, D), 0.5, 3.0, ((0, 32),)),
        "gain_ffn": jnp.clip(1.0 + 0.1 * jax.random.normal(splits[9], (D,), jnp.float32), 0.5, 1.5).astype(jnp.bfloat16),
        "w_gate": normal_values(splits[10], (D, FF), D ** -0.5, 0.21875, ((0, 32),)),
        "w_up": normal_values(splits[11], (D, FF), D ** -0.5, 0.21875, ((0, 32),)),
        "w_down": normal_values(splits[12], (D, FF), (FF // 16) ** -0.5, 0.5, ((0, 32),)),
    }


BRANCH_SCALE = 1.4 / math.sqrt(40.0)
NORM_EPS = 1e-05
MASKED = -1e+30
HIGHEST = lax.Precision.HIGHEST

@jax.custom_vjp
def low(v):
    return lax.optimization_barrier(v.astype(jnp.bfloat16)).astype(jnp.float32)

@jax.custom_vjp
def low_back(v):
    return v

def low_keep(v):
    return (low(v), None)

def low_pass(kept, grad):
    return (grad,)

def back_keep(v):
    return (v, None)

def back_low(kept, grad):
    return (low(grad),)
low.defvjp(low_keep, low_pass)
low_back.defvjp(back_keep, back_low)

def stretch_positions(stretch_order, seq_len):
    stretch_len = seq_len // stretch_order.shape[0]
    row_ids = jnp.arange(seq_len, dtype=jnp.int32)
    return stretch_order[row_ids // stretch_len] * stretch_len + row_ids % stretch_len

def rotate(values, positions):
    half_dim = HEAD_DIM // 2
    freqs = jnp.exp(jnp.arange(half_dim, dtype=jnp.float32) * (-2.0 * math.log(10000.0) / HEAD_DIM))
    angles = positions.astype(jnp.float32)[:, None] * freqs[None, :]
    cosine = jnp.cos(angles)[:, None, :]
    sine_part = jnp.sin(angles)[:, None, :]
    first = values[..., :half_dim]
    second = values[..., half_dim:]
    return jnp.concatenate([first * cosine - second * sine_part, second * cosine + first * sine_part], axis=-1)

def rms_scale(values):
    return values * lax.rsqrt(lax.optimization_barrier(jnp.mean(values * values, axis=-1, keepdims=True)) + NORM_EPS)

def attention(queries, keys_all, values_all, positions, length):
    seq_len = queries.shape[0]
    block_rows = math.gcd(seq_len, 512)
    query_blocks = queries.reshape(seq_len // block_rows, block_rows, HEADS, HEAD_DIM)
    pos_blocks = positions.reshape(seq_len // block_rows, block_rows)
    key_live = positions < length
    score_scale = HEAD_DIM ** (-0.5)

    def one_block(block_pair):
        query_part, query_pos = block_pair
        scores = low_back(jnp.einsum('qhd,khd->hqk', query_part, keys_all, precision=HIGHEST) * score_scale)
        allowed = (positions[None, :] <= query_pos[:, None]) & key_live[None, :]
        scores = jnp.where(allowed[None], scores, MASKED)
        shifted = jnp.exp(scores - lax.optimization_barrier(jnp.max(scores, axis=-1, keepdims=True)))
        attend = shifted / lax.optimization_barrier(jnp.sum(shifted, axis=-1, keepdims=True))
        return jnp.einsum('hqk,khd->qhd', low(attend), values_all, precision=HIGHEST)
    outputs = lax.map(jax.checkpoint(one_block), (query_blocks, pos_blocks))
    return outputs.reshape(seq_len, HEADS * HEAD_DIM)

def layer(tokens, length, positions, params):
    gain_attn, w_query, w_key, w_value, w_out, gain_ffn, w_gate, w_up, w_down = params
    seq_len = tokens.shape[0]
    normed = low(rms_scale(tokens) * gain_attn)
    query_lin = low_back(jnp.dot(normed, w_query, precision=HIGHEST))
    key_lin = low_back(jnp.dot(normed, w_key, precision=HIGHEST))
    queries = low_back(low(rotate(query_lin.reshape(seq_len, HEADS, HEAD_DIM), positions)))
    keys_all = low_back(low(rotate(key_lin.reshape(seq_len, HEADS, HEAD_DIM), positions)))
    values_all = low_back(low(jnp.dot(normed, w_value, precision=HIGHEST))).reshape(seq_len, HEADS, HEAD_DIM)
    mixed = low_back(low(attention(queries, keys_all, values_all, positions, length)))
    branch = low_back(jnp.dot(mixed, w_out, precision=HIGHEST))
    middle = tokens + BRANCH_SCALE * branch
    normed_ffn = low(rms_scale(middle) * gain_ffn)
    gate_act = low_back(jnp.dot(normed_ffn, w_gate, precision=HIGHEST))
    upward = low_back(jnp.dot(normed_ffn, w_up, precision=HIGHEST))
    hidden = low(jax.nn.silu(gate_act) * upward)
    down_out = low_back(jnp.dot(hidden, w_down.T, precision=HIGHEST))
    return middle + BRANCH_SCALE * down_out

def reference(tokens, cotangent, lengths, stretch_order, gain_attn, w_query, w_key, w_value, w_out, gain_ffn, w_gate, w_up, w_down):
    seq_count = lengths.shape[0]
    width = tokens.shape[1]
    seq_len = tokens.shape[0] // seq_count
    positions = stretch_positions(stretch_order, seq_len)
    params = tuple((weight.astype(jnp.float32) for weight in (gain_attn, w_query, w_key, w_value, w_out, gain_ffn, w_gate, w_up, w_down)))
    inputs = tokens.astype(jnp.float32).reshape(seq_count, seq_len, width)

    def forward(values, weights):

        def one_sequence(seq_pair):
            return layer(seq_pair[0], seq_pair[1], positions, weights)
        return lax.map(jax.checkpoint(one_sequence), (values, lengths))
    outputs, pull_back = jax.vjp(forward, inputs, params)
    live = (positions[None, :] < lengths[:, None]).astype(jnp.float32)
    cot_live = cotangent.astype(jnp.float32).reshape(seq_count, seq_len, width) * live[:, :, None]
    grad_tokens, grads = pull_back(cot_live)
    return (outputs.reshape(-1, width), grad_tokens.reshape(-1, width), grads[0], grads[1], grads[2], grads[3], grads[4], grads[5], grads[6], grads[7], grads[8])
```

```python
import functools
import math

import jax
import jax.numpy as jnp
from jax import lax
from jax.experimental import pallas as pl
from jax.experimental.pallas import tpu as pltpu
from jax.sharding import PartitionSpec as P

HEADS = 12
HEAD_DIM = 64

BRANCH_SCALE = 1.4 / math.sqrt(40.0)
NORM_EPS = 1e-05
MASKED = -1e30
SCORE_SCALE = HEAD_DIM ** (-0.5)

ALL = ("dp", "blk", "ulysses")
F32 = jnp.float32
BF16 = jnp.bfloat16


def normalize(values):
    inverse = lax.rsqrt(jnp.mean(values * values, axis=-1, keepdims=True) + NORM_EPS)
    return (values * inverse, inverse)


def norm_back(d_scaled, scaled, inverse):
    return inverse * (d_scaled - scaled * jnp.mean(d_scaled * scaled, axis=-1, keepdims=True))


def dot(left, right, left_dim, right_dim):
    return lax.dot_general(
        left, right, (((left_dim,), (right_dim,)), ((), ())), preferred_element_type=F32
    )


def in_order(flag, mine, other, axis):
    first = jnp.where(flag == 0, mine, other)
    second = jnp.where(flag == 0, other, mine)
    return jnp.stack([first, second], axis=axis)


def roll_to(pieces, shift):
    count = pieces.shape[0]
    doubled = jnp.concatenate([pieces, pieces], axis=0)
    return lax.dynamic_slice_in_dim(doubled, shift, count, 0)


def allowed_block(key_stretch, query_stretch, length, rows):
    key_pos = key_stretch * rows + lax.broadcasted_iota(jnp.int32, (rows, rows), 0)
    query_pos = query_stretch * rows + lax.broadcasted_iota(jnp.int32, (rows, rows), 1)
    return (key_pos <= query_pos) & (key_pos < length)


def flip2(value):
    return jnp.transpose(value)


def forward_kernel(own_count, other_count, group, rows, stretch_ref, length_ref, *refs):
    own = refs[:own_count]
    other = refs[own_count : own_count + other_count]
    out_ref, exact_ref, logsum_ref = refs[own_count + other_count : own_count + other_count + 3]
    q_s, k_s, v_s, top_s, total_s, accum_s = refs[own_count + other_count + 3 :]
    width = group * HEAD_DIM
    key_count = own_count + other_count
    for block in range(key_count):
        if block < own_count:
            source, base = own[block], width
            q_s[block] = source[:width, :]
        else:
            source, base = other[block - own_count], 0
        for head in range(group):
            at = base + head * HEAD_DIM
            k_s[block, head] = flip2(source[at : at + HEAD_DIM, :])
        v_s[block] = source[base + width : base + 2 * width, :]
    length = length_ref[0]

    def step(query_block, key_block, masked):
        if masked:
            allowed = allowed_block(
                stretch_ref[key_block], stretch_ref[query_block], length, rows
            )
        for head in range(group):
            at = head * HEAD_DIM
            scores = jnp.dot(
                k_s[key_block, head],
                q_s[query_block, at : at + HEAD_DIM, :],
                preferred_element_type=F32,
            )
            if masked:
                scores = jnp.where(allowed, scores, MASKED)
            top = top_s[head : head + 1, :]
            top_new = jnp.maximum(top, jnp.max(scores, axis=0, keepdims=True))
            weights = jnp.exp(scores - top_new)
            if masked:
                weights = jnp.where(allowed, weights, 0.0)
            fade = jnp.exp(top - top_new)
            total_s[head : head + 1, :] = total_s[head : head + 1, :] * fade + jnp.sum(
                weights, axis=0, keepdims=True
            )
            top_s[head : head + 1, :] = top_new
            accum_s[at : at + HEAD_DIM, :] = accum_s[at : at + HEAD_DIM, :] * fade + jnp.dot(
                v_s[key_block, at : at + HEAD_DIM, :],
                weights.astype(BF16),
                preferred_element_type=F32,
            )

    def over_queries(query_block, carry):
        top_s[...] = jnp.full(top_s.shape, MASKED, F32)
        total_s[...] = jnp.zeros(total_s.shape, F32)
        accum_s[...] = jnp.zeros(accum_s.shape, F32)
        mine = stretch_ref[query_block]

        def over_keys(key_block, inner):
            theirs = stretch_ref[key_block]
            active = (theirs <= mine) & (theirs * rows < length)
            partial = (theirs == mine) | (theirs * rows + rows > length)

            @pl.when(active & jnp.logical_not(partial))
            def _():
                step(query_block, key_block, False)

            @pl.when(active & partial)
            def _():
                step(query_block, key_block, True)

            return inner

        lax.fori_loop(0, key_count, over_keys, 0)
        for head in range(group):
            at = head * HEAD_DIM
            total = total_s[head : head + 1, :]
            value = accum_s[at : at + HEAD_DIM, :] / total
            exact_ref[query_block, at : at + HEAD_DIM, :] = value
            out_ref[query_block, at : at + HEAD_DIM, :] = value.astype(BF16)
        logsum_ref[query_block] = top_s[...] + jnp.log(total_s[...])
        return carry

    lax.fori_loop(0, own_count, over_queries, 0)


def backward_kernel(own_count, other_count, group, rows, stretch_ref, length_ref, *refs):
    own = refs[:own_count]
    other = refs[own_count : own_count + other_count]
    refs = refs[own_count + other_count :]
    dout = refs[:own_count]
    exact_ref, logsum_ref = refs[own_count : own_count + 2]
    dq_ref, dkv_ref = refs[own_count + 2 : own_count + 4]
    q_s, k_s, kt_s, v_s, do_s, delta_s, dq_s = refs[own_count + 4 :]
    width = group * HEAD_DIM
    key_count = own_count + other_count
    for block in range(key_count):
        if block < own_count:
            source, base = own[block], width
            q_s[block] = source[:width, :]
            do_s[block] = dout[block][...]
            product = dout[block][...].astype(F32) * exact_ref[block]
            for head in range(group):
                at = head * HEAD_DIM
                delta_s[block, head : head + 1, :] = jnp.sum(
                    product[at : at + HEAD_DIM, :], axis=0, keepdims=True
                )
        else:
            source, base = other[block - own_count], 0
        kt_s[block] = source[base : base + width, :]
        for head in range(group):
            at = base + head * HEAD_DIM
            k_s[block, head] = flip2(source[at : at + HEAD_DIM, :])
            v_s[block, head] = flip2(source[at + width : at + width + HEAD_DIM, :])
    dq_s[...] = jnp.zeros(dq_s.shape, F32)
    dkv_ref[...] = jnp.zeros(dkv_ref.shape, F32)
    length = length_ref[0]

    def step(query_block, key_block, masked):
        if masked:
            allowed = allowed_block(
                stretch_ref[key_block], stretch_ref[query_block], length, rows
            )
        for head in range(group):
            at = head * HEAD_DIM
            span = slice(at, at + HEAD_DIM)
            value_span = slice(width + at, width + at + HEAD_DIM)
            q_t = q_s[query_block, span, :]
            do_t = do_s[query_block, span, :]
            scores = jnp.dot(k_s[key_block, head], q_t, preferred_element_type=F32)
            attend = jnp.exp(scores - logsum_ref[query_block, head : head + 1, :])
            if masked:
                attend = jnp.where(allowed, attend, 0.0)
            d_attend = jnp.dot(v_s[key_block, head], do_t, preferred_element_type=F32)
            d_scores = (attend * (d_attend - delta_s[query_block, head : head + 1, :])).astype(BF16)
            dkv_ref[key_block, value_span, :] += dot(do_t, attend.astype(BF16), 1, 1)
            dkv_ref[key_block, span, :] += dot(q_t, d_scores, 1, 1)
            dq_s[query_block, span, :] += jnp.dot(
                kt_s[key_block, span, :], d_scores, preferred_element_type=F32
            )

    def over_queries(query_block, carry):
        mine = stretch_ref[query_block]

        def over_keys(key_block, inner):
            theirs = stretch_ref[key_block]
            live = mine * rows < length

            @pl.when(live & (theirs < mine))
            def _():
                step(query_block, key_block, False)

            @pl.when(live & (theirs == mine))
            def _():
                step(query_block, key_block, True)

            return inner

        return lax.fori_loop(0, key_count, over_keys, carry)

    lax.fori_loop(0, own_count, over_queries, 0)
    for block in range(own_count):
        dq_ref[block] = (dq_s[block] * SCORE_SCALE).astype(BF16)


def in_smem():
    return pl.BlockSpec(memory_space=pltpu.SMEM)


def in_vmem():
    return pl.BlockSpec(memory_space=pltpu.VMEM)


def attention_forward(stretches, length, own, other, group):
    rows = own[0].shape[1]
    width = group * HEAD_DIM
    count, extra = len(own), len(other)
    blocks = count + extra
    return pl.pallas_call(
        functools.partial(forward_kernel, count, extra, group, rows),
        out_shape=(
            jax.ShapeDtypeStruct((count, width, rows), BF16),
            jax.ShapeDtypeStruct((count, width, rows), F32),
            jax.ShapeDtypeStruct((count, 8, rows), F32),
        ),
        in_specs=[in_smem()] * 2 + [in_vmem()] * blocks,
        out_specs=(in_vmem(),) * 3,
        scratch_shapes=[
            pltpu.VMEM((count, width, rows), BF16),
            pltpu.VMEM((blocks, group, rows, HEAD_DIM), BF16),
            pltpu.VMEM((blocks, width, rows), BF16),
            pltpu.VMEM((8, rows), F32),
            pltpu.VMEM((8, rows), F32),
            pltpu.VMEM((width, rows), F32),
        ],
        name="attention_forward",
    )(stretches, length, *own, *other)


def attention_backward(stretches, length, own, other, dout, exact, logsum, group):
    rows = own[0].shape[1]
    width = group * HEAD_DIM
    count, extra = len(own), len(other)
    blocks = count + extra
    return pl.pallas_call(
        functools.partial(backward_kernel, count, extra, group, rows),
        out_shape=(
            jax.ShapeDtypeStruct((count, width, rows), BF16),
            jax.ShapeDtypeStruct((blocks, 2 * width, rows), F32),
        ),
        in_specs=[in_smem()] * 2 + [in_vmem()] * (blocks + count + 2),
        out_specs=(in_vmem(),) * 2,
        scratch_shapes=[
            pltpu.VMEM((count, width, rows), BF16),
            pltpu.VMEM((blocks, group, rows, HEAD_DIM), BF16),
            pltpu.VMEM((blocks, width, rows), BF16),
            pltpu.VMEM((blocks, group, rows, HEAD_DIM), BF16),
            pltpu.VMEM((count, width, rows), BF16),
            pltpu.VMEM((count, 8, rows), F32),
            pltpu.VMEM((count, width, rows), F32),
        ],
        name="attention_backward",
    )(stretches, length, *own, *other, *dout, exact, logsum)


def local(
    tokens,
    cotangent,
    lengths,
    stretch_order,
    gain_attn,
    w_query,
    w_key,
    w_value,
    w_out,
    gain_ffn,
    w_gate,
    w_up,
    w_down,
):
    rows, width = tokens.shape
    hidden_units = w_gate.shape[1]
    shard = w_query.shape[0]
    blk_size = lax.axis_size("blk")
    uly_size = lax.axis_size("ulysses")
    dp_size = lax.axis_size("dp")
    assert dp_size == 4 and uly_size == 2
    head_parts = math.gcd(HEADS, blk_size)
    group = HEADS // head_parts
    part_width = group * HEAD_DIM
    members = (blk_size // head_parts) * uly_size
    stretch_count = stretch_order.shape[0]
    assert stretch_count == blk_size * uly_size

    dp_at = lax.axis_index("dp")
    blk_at = lax.axis_index("blk")
    uly_at = lax.axis_index("ulysses")
    x_at, core_at = dp_at // 2, dp_at % 2
    part_at = blk_at % head_parts
    member_at = (blk_at // head_parts) * uly_size + uly_at

    def over_core(value):
        return lax.ppermute(value, "dp", [(i, i ^ 1) for i in range(dp_size)])

    def over_x(value):
        return lax.ppermute(value, "dp", [(i, i ^ 2) for i in range(dp_size)])

    def over_y(value):
        return lax.ppermute(value, "ulysses", [(i, i ^ 1) for i in range(uly_size)])

    def over_blk(value, shift):
        return lax.ppermute(value, "blk", [(i, (i + shift) % blk_size) for i in range(blk_size)])

    def over_part(value, shift):
        return lax.ppermute(
            value,
            "blk",
            [
                (i, i - i % head_parts + (i + shift) % head_parts)
                for i in range(blk_size)
            ],
        )

    def over_member(value, shift):
        pairs = []
        for source in range(blk_size * uly_size):
            blk, uly = divmod(source, uly_size)
            member = (blk // head_parts) * uly_size + uly
            target = (member + shift) % members
            new_blk = (target // uly_size) * head_parts + blk % head_parts
            pairs.append((source, new_blk * uly_size + target % uly_size))
        return lax.ppermute(value, ("blk", "ulysses"), pairs)

    labels = jnp.arange(stretch_count, dtype=jnp.int32)
    places = []
    for member_shift in range(members):
        for part_shift in range(head_parts):
            member = (member_at - member_shift) % members
            part = (part_at - part_shift) % head_parts
            block = (member // uly_size) * head_parts + part
            places.append(block * uly_size + member % uly_size)
    places = jnp.stack(places).astype(jnp.int32)
    stretches = jnp.sum(
        jnp.where(places[:, None] == labels[None, :], stretch_order[None, :], 0), axis=1
    ).astype(jnp.int32)
    length = lengths[0]

    own_pos = stretches[0] * rows + jnp.arange(rows, dtype=jnp.int32)
    half_dim = HEAD_DIM // 2
    freqs = jnp.exp(jnp.arange(half_dim, dtype=F32) * (-2.0 * math.log(10000.0) / HEAD_DIM))
    angles = freqs[:, None] * own_pos.astype(F32)[None, :]
    cosine, sine_part = jnp.cos(angles), jnp.sin(angles)

    def rotate(values, direction):
        first = values[..., :half_dim, :]
        second = values[..., half_dim:, :]
        return jnp.concatenate(
            [
                first * cosine - direction * second * sine_part,
                second * cosine + direction * first * sine_part,
            ],
            axis=-2,
        )

    def by_part(part):
        span = slice(part * part_width, (part + 1) * part_width)
        return [w_query[:, span], w_key[:, span], w_value[:, span]]

    gains = jnp.pad(jnp.stack([gain_attn, gain_ffn], axis=1), ((0, 0), (0, 126)))
    qkv_local = jnp.concatenate(
        [gains] + [w for part in range(head_parts) for w in by_part(part)], axis=1
    )
    first_columns = 128 + 3 * width // 2
    arrived = [qkv_local] + [over_blk(qkv_local, shift) for shift in range(1, blk_size)]
    backwards = jnp.stack([arrived[(-i) % blk_size] for i in range(blk_size)])
    gathered = roll_to(backwards, (blk_size - blk_at) % blk_size)
    half_a, half_b = gathered[..., :first_columns], gathered[..., first_columns:]
    half_a, half_b = lax.optimization_barrier((half_a, half_b))
    a_x = over_x(half_a)
    b_y = over_y(half_b)
    a_y = over_y(half_a)
    b_x = over_x(half_b)
    a_xy = over_y(a_x)
    b_xy = over_x(b_y)

    def plane(mine, by_x, by_y, by_xy):
        return in_order(
            x_at, in_order(uly_at, mine, by_y, 1), in_order(uly_at, by_x, by_xy, 1), 0
        )

    core_half = jnp.concatenate(
        [plane(half_a, a_x, a_y, a_xy), plane(half_b, b_x, b_y, b_xy)], axis=-1
    )
    core_half = lax.optimization_barrier(core_half)
    core_other = over_core(core_half)
    qkv_all = in_order(core_at, core_half, core_other, 1).reshape(width, -1)
    gain_attn_all = qkv_all[:, 0].astype(F32)
    gain_ffn_all = qkv_all[:, 1].astype(F32)
    w_qkv = qkv_all[:, 128:]

    rest_local = jnp.concatenate([w_out, w_down, w_gate, w_up], axis=1)
    rest_local, _ = lax.optimization_barrier((rest_local, a_x))
    rest_all = lax.all_gather(rest_local, ALL, axis=0, tiled=True)
    out_all = rest_all[:, :width]
    down_all = rest_all[:, width : width + hidden_units]
    gate_up_all = rest_all[:, width + hidden_units :]

    inputs = tokens.astype(F32)
    scaled_in, inverse_in = normalize(inputs)
    normed_attn = (scaled_in * gain_attn_all[None, :]).astype(BF16)
    qkv_lin = dot(w_qkv, normed_attn, 0, 1).reshape(
        head_parts, 3, group, HEAD_DIM, rows
    )
    qkv_send = jnp.stack(
        [
            (rotate(qkv_lin[:, 0], 1.0).astype(BF16) * SCORE_SCALE).astype(BF16),
            rotate(qkv_lin[:, 1], 1.0).astype(BF16),
            qkv_lin[:, 2].astype(BF16),
        ],
        axis=1,
    ).reshape(head_parts, 3 * part_width, rows)

    def scatter_parts(pieces):
        result = []
        for shift in range(head_parts):
            piece = lax.dynamic_index_in_dim(
                pieces, (part_at + shift) % head_parts, 0, keepdims=False
            )
            result.append(over_part(piece, shift) if shift else piece)
        return result

    def return_parts(pieces):
        back = [
            over_part(piece, head_parts - shift) if shift else piece
            for shift, piece in enumerate(pieces)
        ]
        return roll_to(jnp.stack(back), (head_parts - part_at) % head_parts)

    own = scatter_parts(qkv_send)
    other = [
        over_member(piece[part_width:], member_shift)
        for member_shift in range(1, members)
        for piece in own
    ]
    out_t, exact_t, logsum = attention_forward(stretches, lengths, own, other, group)
    attn_t = return_parts([out_t[i] for i in range(head_parts)]).reshape(width, rows)

    middle = inputs + BRANCH_SCALE * dot(attn_t, out_all, 0, 0)
    scaled_mid, inverse_mid = normalize(middle)
    normed_ffn = (scaled_mid * gain_ffn_all[None, :]).astype(BF16)
    gate_up = dot(normed_ffn, gate_up_all, 1, 0)
    gate_act = gate_up[:, :hidden_units]
    upward = gate_up[:, hidden_units:]
    sigma = jax.nn.sigmoid(gate_act)
    silu_act = gate_act * sigma
    hidden = (silu_act * upward).astype(BF16)
    output = middle + BRANCH_SCALE * dot(hidden, down_all, 1, 1)

    live = (own_pos < length).astype(F32)
    d_out = cotangent.astype(F32) * live[:, None]
    d_down = (BRANCH_SCALE * d_out).astype(BF16)
    d_hidden = dot(d_down, down_all, 1, 0)
    d_gate = (d_hidden * upward * sigma * (1.0 + gate_act * (1.0 - sigma))).astype(BF16)
    d_up = (d_hidden * silu_act).astype(BF16)
    d_gate_up = jnp.concatenate([d_gate, d_up], axis=1)
    d_normed_ffn = dot(d_gate_up, gate_up_all, 1, 1)
    d_middle = d_out + norm_back(d_normed_ffn * gain_ffn_all[None, :], scaled_mid, inverse_mid)
    d_branch = (BRANCH_SCALE * d_middle).astype(BF16)
    d_attn_t = dot(out_all, d_branch, 1, 1).astype(BF16)
    dout = scatter_parts(d_attn_t.reshape(head_parts, part_width, rows))

    rest_grads = jnp.concatenate(
        [
            dot(attn_t, d_branch, 1, 0).astype(BF16),
            dot(d_down, hidden, 0, 0).astype(BF16),
            dot(normed_ffn, d_gate_up, 0, 0).astype(BF16),
            jnp.pad(
                jnp.sum(d_normed_ffn * scaled_mid, axis=0)[:, None], ((0, 0), (0, 127))
            ).astype(BF16),
        ],
        axis=1,
    )
    rest_sum = lax.psum_scatter(rest_grads, ALL, scatter_dimension=0, tiled=True).astype(F32)

    dq_t, dkv_t = attention_backward(
        stretches, lengths, own, other, dout, exact_t, logsum, group
    )
    back = []
    for shift in range(head_parts):
        total = dkv_t[shift]
        for member_shift in range(1, members):
            theirs = dkv_t[member_shift * head_parts + shift].astype(BF16)
            total = total + over_member(theirs, members - member_shift).astype(F32)
        back.append(jnp.concatenate([dq_t[shift], total.astype(BF16)], axis=0))
    d_qkv = return_parts(back).reshape(head_parts, 3, group, HEAD_DIM, rows)
    d_qkv_t = jnp.stack(
        [
            rotate(d_qkv[:, 0].astype(F32), -1.0).astype(BF16),
            rotate(d_qkv[:, 1].astype(F32), -1.0).astype(BF16),
            d_qkv[:, 2],
        ],
        axis=1,
    ).reshape(3 * width, rows)

    d_normed = dot(d_qkv_t, w_qkv, 0, 1)
    d_inputs = d_middle + norm_back(d_normed * gain_attn_all[None, :], scaled_in, inverse_in)

    def relative(values):
        tail = values.shape[1:]
        grid = values.reshape((2, 2, blk_size, 2, shard) + tail)
        grid = jnp.where(x_at == 0, grid, grid[::-1])
        grid = jnp.where(core_at == 0, grid, grid[:, ::-1])
        grid = jnp.where(uly_at == 0, grid, grid[:, :, :, ::-1])
        grid = jnp.transpose(grid, (2, 1, 0, 3, 4) + tuple(range(5, grid.ndim)))
        reverse = jnp.stack([grid[(-i) % blk_size] for i in range(blk_size)])
        rolled = roll_to(reverse, (blk_size - blk_at) % blk_size)
        return jnp.transpose(rolled, (1, 2, 3, 0, 4) + tuple(range(5, grid.ndim)))

    gain_column = jnp.sum(d_normed * scaled_in, axis=0)
    left = relative(jnp.transpose(normed_attn))
    gain_left = relative(gain_column[:, None])
    rows_per_core = width // 2

    def qkv_grads(core):
        return jnp.concatenate(
            [
                jnp.pad(gain_left[core].reshape(rows_per_core, 1), ((0, 0), (0, 127))),
                dot(left[core].reshape(rows_per_core, rows), d_qkv_t, 1, 1),
            ],
            axis=1,
        )

    far = over_core(qkv_grads(1).astype(BF16))
    near = (qkv_grads(0) + far.astype(F32)).astype(BF16)
    near = near.reshape(2, 2, blk_size, shard, -1)
    part_a, part_b = near[..., :first_columns], near[..., first_columns:]
    a_from_x = over_x(part_a[1])
    b_from_y = over_y(part_b[:, 1])
    part_a = (part_a[0].astype(F32) + a_from_x.astype(F32)).astype(BF16)
    part_b = (part_b[:, 0].astype(F32) + b_from_y.astype(F32)).astype(BF16)
    a_from_y = over_y(part_a[1])
    b_from_x = over_x(part_b[1])
    joined = jnp.concatenate(
        [
            part_a[0].astype(F32) + a_from_y.astype(F32),
            part_b[0].astype(F32) + b_from_x.astype(F32),
        ],
        axis=-1,
    )
    total = joined[0]
    for shift in range(1, blk_size):
        total = total + over_blk(joined[shift].astype(BF16), blk_size - shift).astype(F32)
    grad_parts = total[:, 128:].reshape(shard, head_parts, 3, part_width)
    grad_qkv = jnp.transpose(grad_parts, (2, 0, 1, 3)).reshape(3, shard, width)

    gate_base = width + hidden_units
    return (
        output,
        d_inputs,
        total[:, 0],
        grad_qkv[0],
        grad_qkv[1],
        grad_qkv[2],
        rest_sum[:, :width],
        rest_sum[:, gate_base + 2 * hidden_units],
        rest_sum[:, gate_base : gate_base + hidden_units],
        rest_sum[:, gate_base + hidden_units : gate_base + 2 * hidden_units],
        rest_sum[:, width:gate_base],
    )


def solution(mesh):
    row, flat = P(ALL, None), P(ALL)
    in_specs = (row, row, P("dp"), P(), flat, row, row, row, row, flat, row, row, row)
    out_specs = (row, row, flat, row, row, row, row, flat, row, row, row)
    return jax.shard_map(local, mesh=mesh, in_specs=in_specs, out_specs=out_specs, check_vma=False)
```

```python
import functools
import math

import jax
import jax.numpy as jnp
from jax import lax
from jax.experimental import pallas as pl
from jax.experimental.pallas import tpu as pltpu
from jax.sharding import PartitionSpec as P


HEADS = 12
HEAD_DIM = 64

BRANCH_SCALE = 1.4 / math.sqrt(40.0)
NORM_EPS = 1e-05
MASKED = -1e30
SCORE_SCALE = HEAD_DIM ** (-0.5)

ALL = ("dp", "blk", "ulysses")
F32 = jnp.float32
BF16 = jnp.bfloat16


def after(value, *earlier):
    return lax.optimization_barrier((value,) + earlier)[0]


def normalize(values):
    inverse = lax.rsqrt(jnp.mean(values * values, axis=-1, keepdims=True) + NORM_EPS)
    return (values * inverse, inverse)


def norm_back(d_scaled, scaled, inverse):
    return inverse * (d_scaled - scaled * jnp.mean(d_scaled * scaled, axis=-1, keepdims=True))


def dot(left, right, left_dim, right_dim):
    return lax.dot_general(
        left, right, (((left_dim,), (right_dim,)), ((), ())), preferred_element_type=F32
    )


def in_order(flag, mine, other, axis):
    first = jnp.where(flag == 0, mine, other)
    second = jnp.where(flag == 0, other, mine)
    return jnp.stack([first, second], axis=axis)


def roll_to(pieces, shift):
    count = pieces.shape[0]
    doubled = jnp.concatenate([pieces, pieces], axis=0)
    return lax.dynamic_slice_in_dim(doubled, shift, count, 0)


def allowed_block(key_stretch, query_stretch, length, rows):
    key_pos = key_stretch * rows + lax.broadcasted_iota(jnp.int32, (rows, rows), 0)
    query_pos = query_stretch * rows + lax.broadcasted_iota(jnp.int32, (rows, rows), 1)
    return (key_pos <= query_pos) & (key_pos < length)


def flip2(value):
    return jnp.transpose(value)


def forward_kernel(own_count, other_count, group, rows, stretch_ref, length_ref, *refs):
    key_count = own_count + other_count
    queries, refs = refs[:own_count], refs[own_count:]
    keys, refs = refs[:key_count], refs[key_count:]
    outs, refs = refs[:own_count], refs[own_count:]
    exact_ref, logsum_ref, q_s, k_s, v_s, out_s, top_s, total_s, accum_s = refs
    width = group * HEAD_DIM
    for block in range(key_count):
        if block < own_count:
            q_s[block] = queries[block][...]
        for head in range(group):
            at = head * HEAD_DIM
            k_s[block, head] = flip2(keys[block][at : at + HEAD_DIM, :])
        v_s[block] = keys[block][width:, :]
    length = length_ref[0]

    def step(query_block, key_block, masked):
        if masked:
            allowed = allowed_block(
                stretch_ref[key_block], stretch_ref[query_block], length, rows
            )
        heads = range(group)
        spans = [slice(head * HEAD_DIM, (head + 1) * HEAD_DIM) for head in heads]
        scores = [
            jnp.dot(
                k_s[key_block, head], q_s[query_block, spans[head], :], preferred_element_type=F32
            )
            for head in heads
        ]
        tops, totals = top_s[...], total_s[...]
        new_tops, new_totals, products, fades = [], [], [], []
        for head in heads:
            score = jnp.where(allowed, scores[head], MASKED) if masked else scores[head]
            top = tops[head : head + 1, :]
            top_new = jnp.maximum(top, jnp.max(score, axis=0, keepdims=True))
            weights = jnp.exp(score - top_new)
            if masked:
                weights = jnp.where(allowed, weights, 0.0)
            fade = jnp.exp(top - top_new)
            new_tops.append(top_new)
            new_totals.append(
                totals[head : head + 1, :] * fade + jnp.sum(weights, axis=0, keepdims=True)
            )
            fades.append(fade)
            products.append(
                jnp.dot(
                    v_s[key_block, spans[head], :],
                    weights.astype(BF16),
                    preferred_element_type=F32,
                )
            )
        for head in heads:
            top_s[head : head + 1, :] = new_tops[head]
            total_s[head : head + 1, :] = new_totals[head]
            accum_s[spans[head], :] = accum_s[spans[head], :] * fades[head] + products[head]

    def over_queries(query_block, carry):
        top_s[...] = jnp.full(top_s.shape, MASKED, F32)
        total_s[...] = jnp.zeros(total_s.shape, F32)
        accum_s[...] = jnp.zeros(accum_s.shape, F32)
        mine = stretch_ref[query_block]

        def over_keys(key_block, inner):
            theirs = stretch_ref[key_block]
            active = (theirs <= mine) & (theirs * rows < length)
            partial = (theirs == mine) | (theirs * rows + rows > length)

            @pl.when(active & jnp.logical_not(partial))
            def _():
                step(query_block, key_block, False)

            @pl.when(active & partial)
            def _():
                step(query_block, key_block, True)

            return inner

        lax.fori_loop(0, key_count, over_keys, 0)
        for head in range(group):
            at = head * HEAD_DIM
            total = total_s[head : head + 1, :]
            value = accum_s[at : at + HEAD_DIM, :] / total
            exact_ref[query_block, at : at + HEAD_DIM, :] = value
            out_s[query_block, at : at + HEAD_DIM, :] = value.astype(BF16)
        logsum_ref[query_block] = top_s[...] + jnp.log(total_s[...])
        return carry

    lax.fori_loop(0, own_count, over_queries, 0)
    for block in range(own_count):
        outs[block][...] = out_s[block]


def backward_kernel(own_count, other_count, group, rows, stretch_ref, length_ref, *refs):
    key_count = own_count + other_count
    queries, refs = refs[:own_count], refs[own_count:]
    keys, refs = refs[:key_count], refs[key_count:]
    douts, refs = refs[:own_count], refs[own_count:]
    (exact_ref, logsum_ref), refs = refs[:2], refs[2:]
    dq_outs, refs = refs[:own_count], refs[own_count:]
    dkv_outs, refs = refs[:key_count], refs[key_count:]
    q_s, k_s, kt_s, v_s, do_s, delta_s, dq_s, dkv_s = refs
    width = group * HEAD_DIM
    for block in range(key_count):
        if block < own_count:
            q_s[block] = queries[block][...]
            do_s[block] = douts[block][...]
            product = douts[block][...].astype(F32) * exact_ref[block]
            for head in range(group):
                at = head * HEAD_DIM
                delta_s[block, head : head + 1, :] = jnp.sum(
                    product[at : at + HEAD_DIM, :], axis=0, keepdims=True
                )
        kt_s[block] = keys[block][:width, :]
        for head in range(group):
            at = head * HEAD_DIM
            k_s[block, head] = flip2(keys[block][at : at + HEAD_DIM, :])
            v_s[block, head] = flip2(keys[block][at + width : at + width + HEAD_DIM, :])
    dq_s[...] = jnp.zeros(dq_s.shape, F32)
    dkv_s[...] = jnp.zeros(dkv_s.shape, F32)
    length = length_ref[0]

    def step(query_block, key_block, masked):
        if masked:
            allowed = allowed_block(
                stretch_ref[key_block], stretch_ref[query_block], length, rows
            )
        heads = range(group)
        spans = [slice(head * HEAD_DIM, (head + 1) * HEAD_DIM) for head in heads]
        q_t = [q_s[query_block, span, :] for span in spans]
        do_t = [do_s[query_block, span, :] for span in spans]
        scores = [
            jnp.dot(k_s[key_block, head], q_t[head], preferred_element_type=F32) for head in heads
        ]
        d_attends = [
            jnp.dot(v_s[key_block, head], do_t[head], preferred_element_type=F32) for head in heads
        ]
        logsums, deltas = logsum_ref[query_block], delta_s[query_block]
        dks, dvs, dqs = [], [], []
        for head in heads:
            attend = jnp.exp(scores[head] - logsums[head : head + 1, :])
            if masked:
                attend = jnp.where(allowed, attend, 0.0)
            d_scores = (attend * (d_attends[head] - deltas[head : head + 1, :])).astype(BF16)
            dvs.append(dot(do_t[head], attend.astype(BF16), 1, 1))
            dks.append(dot(q_t[head], d_scores, 1, 1))
            dqs.append(
                jnp.dot(kt_s[key_block, spans[head], :], d_scores, preferred_element_type=F32)
            )
        dkv_s[key_block] += jnp.concatenate(dks + dvs, axis=0)
        dq_s[query_block] += jnp.concatenate(dqs, axis=0)

    def over_queries(query_block, carry):
        mine = stretch_ref[query_block]

        def over_keys(key_block, inner):
            theirs = stretch_ref[key_block]
            live = mine * rows < length

            @pl.when(live & (theirs < mine))
            def _():
                step(query_block, key_block, False)

            @pl.when(live & (theirs == mine))
            def _():
                step(query_block, key_block, True)

            return inner

        return lax.fori_loop(0, key_count, over_keys, carry)

    lax.fori_loop(0, own_count, over_queries, 0)
    for block in range(own_count):
        dq_outs[block][...] = (dq_s[block] * SCORE_SCALE).astype(BF16)
    for block in range(key_count):
        dkv_outs[block][...] = dkv_s[block].astype(dkv_outs[block].dtype)


def in_smem():
    return pl.BlockSpec(memory_space=pltpu.SMEM)


def in_vmem():
    return pl.BlockSpec(memory_space=pltpu.VMEM)


def attention_forward(stretches, length, queries, keys, group):
    rows = queries[0].shape[1]
    width = group * HEAD_DIM
    count, blocks = len(queries), len(keys)
    outs = pl.pallas_call(
        functools.partial(forward_kernel, count, blocks - count, group, rows),
        out_shape=(jax.ShapeDtypeStruct((width, rows), BF16),) * count
        + (
            jax.ShapeDtypeStruct((count, width, rows), F32),
            jax.ShapeDtypeStruct((count, 8, rows), F32),
        ),
        in_specs=[in_smem()] * 2 + [in_vmem()] * (count + blocks),
        out_specs=(in_vmem(),) * (count + 2),
        scratch_shapes=[
            pltpu.VMEM((count, width, rows), BF16),
            pltpu.VMEM((blocks, group, rows, HEAD_DIM), BF16),
            pltpu.VMEM((blocks, width, rows), BF16),
            pltpu.VMEM((count, width, rows), BF16),
            pltpu.VMEM((8, rows), F32),
            pltpu.VMEM((8, rows), F32),
            pltpu.VMEM((width, rows), F32),
        ],
        name="attention_forward",
    )(stretches, length, *queries, *keys)
    return outs[:count], outs[count], outs[count + 1]


def attention_backward(stretches, length, queries, keys, douts, exact, logsum, group):
    rows = queries[0].shape[1]
    width = group * HEAD_DIM
    count, blocks = len(queries), len(keys)
    outs = pl.pallas_call(
        functools.partial(backward_kernel, count, blocks - count, group, rows),
        out_shape=(jax.ShapeDtypeStruct((width, rows), BF16),) * count
        + (jax.ShapeDtypeStruct((2 * width, rows), F32),) * count
        + (jax.ShapeDtypeStruct((2 * width, rows), BF16),) * (blocks - count),
        in_specs=[in_smem()] * 2 + [in_vmem()] * (2 * count + blocks + 2),
        out_specs=(in_vmem(),) * (count + blocks),
        scratch_shapes=[
            pltpu.VMEM((count, width, rows), BF16),
            pltpu.VMEM((blocks, group, rows, HEAD_DIM), BF16),
            pltpu.VMEM((blocks, width, rows), BF16),
            pltpu.VMEM((blocks, group, rows, HEAD_DIM), BF16),
            pltpu.VMEM((count, width, rows), BF16),
            pltpu.VMEM((count, 8, rows), F32),
            pltpu.VMEM((count, width, rows), F32),
            pltpu.VMEM((blocks, 2 * width, rows), F32),
        ],
        name="attention_backward",
    )(stretches, length, *queries, *keys, *douts, exact, logsum)
    return outs[:count], outs[count:]


def local(
    tokens,
    cotangent,
    lengths,
    stretch_order,
    gain_attn,
    w_query,
    w_key,
    w_value,
    w_out,
    gain_ffn,
    w_gate,
    w_up,
    w_down,
):
    rows, width = tokens.shape
    hidden_units = w_gate.shape[1]
    shard = w_query.shape[0]
    blk_size = lax.axis_size("blk")
    uly_size = lax.axis_size("ulysses")
    dp_size = lax.axis_size("dp")
    assert dp_size == 4 and uly_size == 2
    head_parts = math.gcd(HEADS, blk_size)
    group = HEADS // head_parts
    part_width = group * HEAD_DIM
    members = (blk_size // head_parts) * uly_size
    stretch_count = stretch_order.shape[0]
    assert stretch_count == blk_size * uly_size

    dp_at = lax.axis_index("dp")
    blk_at = lax.axis_index("blk")
    uly_at = lax.axis_index("ulysses")
    x_at, core_at = dp_at // 2, dp_at % 2
    part_at = blk_at % head_parts
    member_at = (blk_at // head_parts) * uly_size + uly_at

    def over_core(value):
        return lax.ppermute(value, "dp", [(i, i ^ 1) for i in range(dp_size)])

    def over_x(value):
        return lax.ppermute(value, "dp", [(i, i ^ 2) for i in range(dp_size)])

    def over_y(value):
        return lax.ppermute(value, "ulysses", [(i, i ^ 1) for i in range(uly_size)])

    def over_blk(value, shift):
        return lax.ppermute(value, "blk", [(i, (i + shift) % blk_size) for i in range(blk_size)])

    def over_part(value, shift):
        return lax.ppermute(
            value,
            "blk",
            [
                (i, i - i % head_parts + (i + shift) % head_parts)
                for i in range(blk_size)
            ],
        )

    def over_member(value, shift):
        pairs = []
        for source in range(blk_size * uly_size):
            blk, uly = divmod(source, uly_size)
            member = (blk // head_parts) * uly_size + uly
            target = (member + shift) % members
            new_blk = (target // uly_size) * head_parts + blk % head_parts
            pairs.append((source, new_blk * uly_size + target % uly_size))
        return lax.ppermute(value, ("blk", "ulysses"), pairs)

    labels = jnp.arange(stretch_count, dtype=jnp.int32)
    places = []
    for member_shift in range(members):
        for part_shift in range(head_parts):
            member = (member_at - member_shift) % members
            part = (part_at - part_shift) % head_parts
            block = (member // uly_size) * head_parts + part
            places.append(block * uly_size + member % uly_size)
    places = jnp.stack(places).astype(jnp.int32)
    stretches = jnp.sum(
        jnp.where(places[:, None] == labels[None, :], stretch_order[None, :], 0), axis=1
    ).astype(jnp.int32)
    length = lengths[0]

    own_pos = stretches[0] * rows + jnp.arange(rows, dtype=jnp.int32)
    half_dim = HEAD_DIM // 2
    freqs = jnp.exp(jnp.arange(half_dim, dtype=F32) * (-2.0 * math.log(10000.0) / HEAD_DIM))
    angles = freqs[:, None] * own_pos.astype(F32)[None, :]
    cosine, sine_part = jnp.cos(angles), jnp.sin(angles)

    def rotate(values, direction):
        first = values[..., :half_dim, :]
        second = values[..., half_dim:, :]
        return jnp.concatenate(
            [
                first * cosine - direction * second * sine_part,
                second * cosine + direction * first * sine_part,
            ],
            axis=-2,
        )

    def plane_first(first, second):
        return over_x(first), over_y(second), over_x(second)

    def plane_second(first, second, first_x, second_y, second_x):
        second_xy = over_x(second_y)
        first_y = over_y(first)
        first_xy = over_y(first_x)
        return (
            plane(first, first_x, first_y, first_xy),
            plane(second, second_x, second_y, second_xy),
        )

    def plane(mine, by_x, by_y, by_xy):
        return in_order(
            x_at, in_order(uly_at, mine, by_y, 1), in_order(uly_at, by_x, by_xy, 1), 0
        )

    def from_line(piece):
        return [piece] + [over_blk(piece, shift) for shift in range(1, blk_size)]

    def line(arrived):
        backwards = jnp.stack([arrived[(-i) % blk_size] for i in range(blk_size)])
        return roll_to(backwards, (blk_size - blk_at) % blk_size)

    def both_cores(half):
        whole = jnp.broadcast_to(half[:, None], half.shape[:1] + (2,) + half.shape[1:])
        start = (0, 1 - core_at) + (0,) * (half.ndim - 1)
        whole = lax.dynamic_update_slice(whole, over_core(half)[:, None], start)
        return whole.reshape(width, -1)

    def by_part(part):
        span = slice(part * part_width, (part + 1) * part_width)
        return [w_key[:, span], w_value[:, span]]

    gains = jnp.pad(jnp.stack([gain_attn, gain_ffn], axis=1), ((0, 0), (0, 126)))
    qkv_local = jnp.concatenate(
        [gains, w_query] + [w for part in range(head_parts) for w in by_part(part)], axis=1
    )
    qkv_line = line(from_line(qkv_local))
    first_columns = 128 + 3 * width // 2
    qkv_halves = lax.optimization_barrier(
        (qkv_line[..., :first_columns], qkv_line[..., first_columns:])
    )
    qkv_firsts = plane_first(*qkv_halves)
    qkv_planes = plane_second(*qkv_halves, *qkv_firsts)
    qkv_half = jnp.concatenate(qkv_planes, axis=-1)
    qkv_all = both_cores(lax.optimization_barrier(qkv_half))
    gain_attn_all = qkv_all[:, 0].astype(F32)
    gain_ffn_all = qkv_all[:, 1].astype(F32)
    w_qkv = qkv_all[:, 128:]

    rest_local = jnp.concatenate([w_down, w_out, w_gate, w_up], axis=1)
    rest_arrived = from_line(after(rest_local, qkv_halves[0]))

    def pick(values, index, axis):
        return lax.dynamic_index_in_dim(values, index, axis, keepdims=False)

    def by_core(left_t):
        grid = left_t.reshape(2, 2, width // 4, rows)
        return tuple(
            pick(grid, core, 1).reshape(width // 2, rows) for core in (1 - core_at, core_at)
        )

    live = (own_pos < length).astype(F32)
    d_out = cotangent.astype(F32) * live[:, None]
    d_down = (BRANCH_SCALE * d_out).astype(BF16)
    inputs = tokens.astype(F32)
    scaled_in, inverse_in = normalize(inputs)
    normed_attn = (scaled_in * gain_attn_all[None, :]).astype(BF16)
    qkv_lin = dot(w_qkv, normed_attn, 0, 1)
    q_lin = qkv_lin[:width].reshape(head_parts, group, HEAD_DIM, rows)
    kv_lin = qkv_lin[width:].reshape(head_parts, 2, group, HEAD_DIM, rows)
    q_send = (rotate(q_lin, 1.0).astype(BF16) * SCORE_SCALE).astype(BF16)
    kv_send = jnp.stack(
        [rotate(kv_lin[:, 0], 1.0).astype(BF16), kv_lin[:, 1].astype(BF16)], axis=1
    )

    def scatter_parts(pieces):
        result = []
        for shift in range(head_parts):
            piece = lax.dynamic_index_in_dim(
                pieces, (part_at + shift) % head_parts, 0, keepdims=False
            )
            result.append(over_part(piece, shift) if shift else piece)
        return result

    def return_parts(pieces, *earlier):
        back = [
            after(over_part(piece, head_parts - shift), *earlier) if shift else piece
            for shift, piece in enumerate(pieces)
        ]
        return roll_to(jnp.stack(back), (head_parts - part_at) % head_parts)

    keys = scatter_parts(kv_send.reshape(head_parts, 2 * part_width, rows))
    queries = scatter_parts(q_send.reshape(head_parts, part_width, rows))
    keys = keys + [
        over_member(piece, member_shift)
        for member_shift in range(1, members)
        for piece in keys
    ]

    rest_arrived = [after(piece, keys[0]) for piece in rest_arrived]
    rest_line = line(rest_arrived)
    rest_halves = lax.optimization_barrier(
        (rest_line[..., :hidden_units], rest_line[..., hidden_units:])
    )
    rest_firsts = plane_first(*rest_halves)
    rest_planes = plane_second(
        *(after(piece, keys[-1]) for piece in rest_halves),
        *(after(piece, keys[-1]) for piece in rest_firsts),
    )
    down_half, other_half = rest_planes

    d_down_rows, normed_rows, lengths = lax.optimization_barrier(
        (by_core(jnp.transpose(d_down)), by_core(jnp.transpose(normed_attn)), lengths)
    )
    outs, exact_t, logsum = attention_forward(stretches, lengths, queries, keys, group)
    down_all = both_cores(lax.optimization_barrier(down_half))
    other_all = both_cores(lax.optimization_barrier(other_half))
    out_all = other_all[:, :width]
    gate_up_all = other_all[:, width:]

    attn_t = return_parts(outs).reshape(width, rows)

    middle = inputs + BRANCH_SCALE * dot(attn_t, out_all, 0, 0)
    scaled_mid, inverse_mid = normalize(middle)
    normed_ffn = (scaled_mid * gain_ffn_all[None, :]).astype(BF16)
    gate_up = dot(normed_ffn, gate_up_all, 1, 0)
    gate_act = gate_up[:, :hidden_units]
    upward = gate_up[:, hidden_units:]
    sigma = jax.nn.sigmoid(gate_act)
    silu_act = gate_act * sigma
    hidden = (silu_act * upward).astype(BF16)
    output = middle + BRANCH_SCALE * dot(hidden, down_all, 1, 1)

    d_hidden = dot(d_down, down_all, 1, 0)
    d_gate = (d_hidden * upward * sigma * (1.0 + gate_act * (1.0 - sigma))).astype(BF16)
    d_up = (d_hidden * silu_act).astype(BF16)
    d_gate_up = jnp.concatenate([d_gate, d_up], axis=1)
    d_normed_ffn = dot(d_gate_up, gate_up_all, 1, 1)
    d_middle = d_out + norm_back(d_normed_ffn * gain_ffn_all[None, :], scaled_mid, inverse_mid)
    d_branch = (BRANCH_SCALE * d_middle).astype(BF16)
    d_attn_t = dot(out_all, d_branch, 1, 1).astype(BF16)
    douts = scatter_parts(d_attn_t.reshape(head_parts, part_width, rows))

    def both(mine, theirs):
        return (mine.astype(F32) + theirs.astype(F32)).astype(BF16)

    def core_sum(left_rows, product):
        far = product(left_rows[0]).astype(BF16)
        near = product(left_rows[1])
        arrived = over_core(far)
        return both(near, arrived).reshape(2, blk_size, 2, shard, -1)

    def x_sum(values, *earlier):
        arrived = over_x(pick(values, 1 - x_at, 0))
        return both(pick(values, x_at, 0), after(arrived, *earlier))

    def y_sum(values, axis, *earlier):
        arrived = over_y(pick(values, 1 - uly_at, axis))
        return both(pick(values, uly_at, axis), after(arrived, *earlier))

    def line_sum(values, *earlier):
        total = pick(values, blk_at, 0).astype(F32)
        for shift in range(1, blk_size):
            piece = pick(values, (blk_at + shift) % blk_size, 0)
            total = total + after(over_blk(piece, shift), *earlier).astype(F32)
        return total

    down_core = core_sum(d_down_rows, lambda l: dot(l, hidden, 1, 0))
    gate_up_core = core_sum(by_core(jnp.transpose(normed_ffn)), lambda l: dot(l, d_gate_up, 1, 0))
    out_core = core_sum(by_core(attn_t), lambda l: dot(l, d_branch, 1, 0))

    dq, dkv = attention_backward(stretches, lengths, queries, keys, douts, exact_t, logsum, group)
    d_q = return_parts(dq).reshape(HEADS, HEAD_DIM, rows)
    d_q_t = rotate(d_q.astype(F32), -1.0).astype(BF16).reshape(width, rows)
    q_core = core_sum(normed_rows, lambda l: dot(l, d_q_t, 1, 1))
    back = []
    for shift in range(head_parts):
        total = dkv[shift]
        for member_shift in range(1, members):
            theirs = dkv[member_shift * head_parts + shift]
            total = total + over_member(theirs, members - member_shift).astype(F32)
        back.append(total.astype(BF16))
    d_kv = return_parts(back, q_core)
    q_x = x_sum(q_core)
    gate_x = x_sum(gate_up_core[..., :hidden_units], back[-1])
    up_y = y_sum(gate_up_core[..., hidden_units:], 2, dkv[0])
    gate_sum = y_sum(gate_x, 1, d_kv)
    up_sum = x_sum(up_y, back[-1])
    down_sum = x_sum(y_sum(down_core, 2, dkv[0]), back[-1])
    out_sum = y_sum(x_sum(out_core, back[-1]), 1, d_kv)
    d_kv = d_kv.reshape(head_parts, 2, group, HEAD_DIM, rows)
    d_kv_t = jnp.stack(
        [rotate(d_kv[:, 0].astype(F32), -1.0).astype(BF16), d_kv[:, 1]], axis=1
    ).reshape(2 * width, rows)

    kv_core = core_sum(normed_rows, lambda l: dot(l, d_kv_t, 1, 1))
    k_x = x_sum(kv_core[..., :width])
    v_y = y_sum(kv_core[..., width:], 2)
    q_sum = y_sum(q_x, 1)
    k_sum = y_sum(k_x, 1)
    v_sum = x_sum(v_y)

    rest_sum = line_sum(jnp.concatenate([down_sum, out_sum, gate_sum, up_sum], axis=-1), q_sum, k_sum, v_sum)
    qkv_sum = line_sum(jnp.concatenate([q_sum, k_sum, v_sum], axis=-1))

    d_normed = dot(d_q_t, w_qkv[:, :width], 0, 1) + dot(d_kv_t, w_qkv[:, width:], 0, 1)
    d_inputs = d_middle + norm_back(d_normed * gain_attn_all[None, :], scaled_in, inverse_in)

    grad_query = qkv_sum[:, :width]
    grad_kv = qkv_sum[:, width:].reshape(shard, head_parts, 2, part_width)
    grad_key = grad_kv[:, :, 0].reshape(shard, width)
    grad_value = grad_kv[:, :, 1].reshape(shard, width)
    grad_down = rest_sum[:, :hidden_units]
    grad_out = rest_sum[:, hidden_units : hidden_units + width]
    grad_gate = rest_sum[:, hidden_units + width : 2 * hidden_units + width]
    grad_up = rest_sum[:, 2 * hidden_units + width :]

    def gain_grad(gain, pairs):
        total = sum(jnp.sum(w.astype(F32) * grad, axis=1) for w, grad in pairs)
        return total / gain.astype(F32)

    return (
        output,
        d_inputs,
        gain_grad(gain_attn, [(w_query, grad_query), (w_key, grad_key), (w_value, grad_value)]),
        grad_query,
        grad_key,
        grad_value,
        grad_out,
        gain_grad(gain_ffn, [(w_gate, grad_gate), (w_up, grad_up)]),
        grad_gate,
        grad_up,
        grad_down,
    )


def solution(mesh):
    row, flat = P(ALL, None), P(ALL)
    in_specs = (row, row, P("dp"), P(), flat, row, row, row, row, flat, row, row, row)
    out_specs = (row, row, flat, row, row, row, row, flat, row, row, row)
    return jax.shard_map(local, mesh=mesh, in_specs=in_specs, out_specs=out_specs, check_vma=False)
```

```python
import functools
import math

import jax
import jax.numpy as jnp
from jax import lax
from jax.experimental import pallas as pl
from jax.experimental.pallas import tpu as pltpu
from jax.sharding import PartitionSpec as P


HEADS = 12
HEAD_DIM = 64

BRANCH_SCALE = 1.4 / math.sqrt(40.0)
NORM_EPS = 1e-05
MASKED = -1e30
SCORE_SCALE = HEAD_DIM ** (-0.5)

ALL = ("dp", "blk", "ulysses")
F32 = jnp.float32
BF16 = jnp.bfloat16


def after(value, *earlier):
    return lax.optimization_barrier((value,) + earlier)[0]


def normalize(values):
    inverse = lax.rsqrt(jnp.mean(values * values, axis=-1, keepdims=True) + NORM_EPS)
    return (values * inverse, inverse)


def norm_back(d_scaled, scaled, inverse):
    return inverse * (d_scaled - scaled * jnp.mean(d_scaled * scaled, axis=-1, keepdims=True))


def dot(left, right, left_dim, right_dim):
    return lax.dot_general(
        left, right, (((left_dim,), (right_dim,)), ((), ())), preferred_element_type=F32
    )


def in_order(flag, mine, other, axis):
    first = jnp.where(flag == 0, mine, other)
    second = jnp.where(flag == 0, other, mine)
    return jnp.stack([first, second], axis=axis)


def roll_to(pieces, shift):
    count = pieces.shape[0]
    doubled = jnp.concatenate([pieces, pieces], axis=0)
    return lax.dynamic_slice_in_dim(doubled, shift, count, 0)


def allowed_block(key_stretch, query_stretch, length, rows):
    key_pos = key_stretch * rows + lax.broadcasted_iota(jnp.int32, (rows, rows), 0)
    query_pos = query_stretch * rows + lax.broadcasted_iota(jnp.int32, (rows, rows), 1)
    return (key_pos <= query_pos) & (key_pos < length)


def flip2(value):
    return jnp.transpose(value)


def forward_kernel(own_count, other_count, group, rows, stretch_ref, length_ref, *refs):
    key_count = own_count + other_count
    queries, refs = refs[:own_count], refs[own_count:]
    keys, refs = refs[:key_count], refs[key_count:]
    outs, refs = refs[:own_count], refs[own_count:]
    exact_ref, logsum_ref, q_s, k_s, v_s, out_s, top_s, total_s, accum_s = refs
    width = group * HEAD_DIM
    for block in range(key_count):
        if block < own_count:
            q_s[block] = queries[block][...]
        for head in range(group):
            at = head * HEAD_DIM
            k_s[block, head] = flip2(keys[block][at : at + HEAD_DIM, :])
        v_s[block] = keys[block][width:, :]
    length = length_ref[0]

    def step(query_block, key_block, masked):
        if masked:
            allowed = allowed_block(
                stretch_ref[key_block], stretch_ref[query_block], length, rows
            )
        heads = range(group)
        spans = [slice(head * HEAD_DIM, (head + 1) * HEAD_DIM) for head in heads]
        scores = [
            jnp.dot(
                k_s[key_block, head], q_s[query_block, spans[head], :], preferred_element_type=F32
            )
            for head in heads
        ]
        tops, totals = top_s[...], total_s[...]
        new_tops, new_totals, products, fades = [], [], [], []
        for head in heads:
            score = jnp.where(allowed, scores[head], MASKED) if masked else scores[head]
            top = tops[head : head + 1, :]
            top_new = jnp.maximum(top, jnp.max(score, axis=0, keepdims=True))
            weights = jnp.exp(score - top_new)
            if masked:
                weights = jnp.where(allowed, weights, 0.0)
            fade = jnp.exp(top - top_new)
            new_tops.append(top_new)
            new_totals.append(
                totals[head : head + 1, :] * fade + jnp.sum(weights, axis=0, keepdims=True)
            )
            fades.append(fade)
            products.append(
                jnp.dot(
                    v_s[key_block, spans[head], :],
                    weights.astype(BF16),
                    preferred_element_type=F32,
                )
            )
        for head in heads:
            top_s[head : head + 1, :] = new_tops[head]
            total_s[head : head + 1, :] = new_totals[head]
            accum_s[spans[head], :] = accum_s[spans[head], :] * fades[head] + products[head]

    def over_queries(query_block, carry):
        top_s[...] = jnp.full(top_s.shape, MASKED, F32)
        total_s[...] = jnp.zeros(total_s.shape, F32)
        accum_s[...] = jnp.zeros(accum_s.shape, F32)
        mine = stretch_ref[query_block]

        def over_keys(key_block, inner):
            theirs = stretch_ref[key_block]
            active = (theirs <= mine) & (theirs * rows < length)
            partial = (theirs == mine) | (theirs * rows + rows > length)

            @pl.when(active & jnp.logical_not(partial))
            def _():
                step(query_block, key_block, False)

            @pl.when(active & partial)
            def _():
                step(query_block, key_block, True)

            return inner

        lax.fori_loop(0, key_count, over_keys, 0)
        for head in range(group):
            at = head * HEAD_DIM
            total = total_s[head : head + 1, :]
            value = accum_s[at : at + HEAD_DIM, :] / total
            exact_ref[query_block, at : at + HEAD_DIM, :] = value
            out_s[query_block, at : at + HEAD_DIM, :] = value.astype(BF16)
        logsum_ref[query_block] = top_s[...] + jnp.log(total_s[...])
        return carry

    lax.fori_loop(0, own_count, over_queries, 0)
    for block in range(own_count):
        outs[block][...] = out_s[block]


def backward_kernel(own_count, other_count, group, rows, stretch_ref, length_ref, *refs):
    key_count = own_count + other_count
    queries, refs = refs[:own_count], refs[own_count:]
    keys, refs = refs[:key_count], refs[key_count:]
    douts, refs = refs[:own_count], refs[own_count:]
    (exact_ref, logsum_ref), refs = refs[:2], refs[2:]
    dq_outs, refs = refs[:own_count], refs[own_count:]
    dkv_outs, refs = refs[:key_count], refs[key_count:]
    q_s, k_s, kt_s, v_s, do_s, delta_s, dq_s, dkv_s = refs
    width = group * HEAD_DIM
    for block in range(key_count):
        if block < own_count:
            q_s[block] = queries[block][...]
            do_s[block] = douts[block][...]
            product = douts[block][...].astype(F32) * exact_ref[block]
            for head in range(group):
                at = head * HEAD_DIM
                delta_s[block, head : head + 1, :] = jnp.sum(
                    product[at : at + HEAD_DIM, :], axis=0, keepdims=True
                )
        kt_s[block] = keys[block][:width, :]
        for head in range(group):
            at = head * HEAD_DIM
            k_s[block, head] = flip2(keys[block][at : at + HEAD_DIM, :])
            v_s[block, head] = flip2(keys[block][at + width : at + width + HEAD_DIM, :])
    dq_s[...] = jnp.zeros(dq_s.shape, F32)
    dkv_s[...] = jnp.zeros(dkv_s.shape, F32)
    length = length_ref[0]

    def step(query_block, key_block, masked):
        if masked:
            allowed = allowed_block(
                stretch_ref[key_block], stretch_ref[query_block], length, rows
            )
        heads = range(group)
        spans = [slice(head * HEAD_DIM, (head + 1) * HEAD_DIM) for head in heads]
        q_t = [q_s[query_block, span, :] for span in spans]
        do_t = [do_s[query_block, span, :] for span in spans]
        scores = [
            jnp.dot(k_s[key_block, head], q_t[head], preferred_element_type=F32) for head in heads
        ]
        d_attends = [
            jnp.dot(v_s[key_block, head], do_t[head], preferred_element_type=F32) for head in heads
        ]
        logsums, deltas = logsum_ref[query_block], delta_s[query_block]
        dks, dvs, dqs = [], [], []
        for head in heads:
            attend = jnp.exp(scores[head] - logsums[head : head + 1, :])
            if masked:
                attend = jnp.where(allowed, attend, 0.0)
            d_scores = (attend * (d_attends[head] - deltas[head : head + 1, :])).astype(BF16)
            dvs.append(dot(do_t[head], attend.astype(BF16), 1, 1))
            dks.append(dot(q_t[head], d_scores, 1, 1))
            dqs.append(
                jnp.dot(kt_s[key_block, spans[head], :], d_scores, preferred_element_type=F32)
            )
        dkv_s[key_block] += jnp.concatenate(dks + dvs, axis=0)
        dq_s[query_block] += jnp.concatenate(dqs, axis=0)

    def over_queries(query_block, carry):
        mine = stretch_ref[query_block]

        def over_keys(key_block, inner):
            theirs = stretch_ref[key_block]
            live = mine * rows < length

            @pl.when(live & (theirs < mine))
            def _():
                step(query_block, key_block, False)

            @pl.when(live & (theirs == mine))
            def _():
                step(query_block, key_block, True)

            return inner

        return lax.fori_loop(0, key_count, over_keys, carry)

    lax.fori_loop(0, own_count, over_queries, 0)
    for block in range(own_count):
        dq_outs[block][...] = (dq_s[block] * SCORE_SCALE).astype(BF16)
    for block in range(key_count):
        dkv_outs[block][...] = dkv_s[block].astype(dkv_outs[block].dtype)


def in_smem():
    return pl.BlockSpec(memory_space=pltpu.SMEM)


def in_vmem():
    return pl.BlockSpec(memory_space=pltpu.VMEM)


def attention_forward(stretches, length, queries, keys, group):
    rows = queries[0].shape[1]
    width = group * HEAD_DIM
    count, blocks = len(queries), len(keys)
    outs = pl.pallas_call(
        functools.partial(forward_kernel, count, blocks - count, group, rows),
        out_shape=(jax.ShapeDtypeStruct((width, rows), BF16),) * count
        + (
            jax.ShapeDtypeStruct((count, width, rows), F32),
            jax.ShapeDtypeStruct((count, 8, rows), F32),
        ),
        in_specs=[in_smem()] * 2 + [in_vmem()] * (count + blocks),
        out_specs=(in_vmem(),) * (count + 2),
        scratch_shapes=[
            pltpu.VMEM((count, width, rows), BF16),
            pltpu.VMEM((blocks, group, rows, HEAD_DIM), BF16),
            pltpu.VMEM((blocks, width, rows), BF16),
            pltpu.VMEM((count, width, rows), BF16),
            pltpu.VMEM((8, rows), F32),
            pltpu.VMEM((8, rows), F32),
            pltpu.VMEM((width, rows), F32),
        ],
        name="attention_forward",
    )(stretches, length, *queries, *keys)
    return outs[:count], outs[count], outs[count + 1]


def attention_backward(stretches, length, queries, keys, douts, exact, logsum, group):
    rows = queries[0].shape[1]
    width = group * HEAD_DIM
    count, blocks = len(queries), len(keys)
    outs = pl.pallas_call(
        functools.partial(backward_kernel, count, blocks - count, group, rows),
        out_shape=(jax.ShapeDtypeStruct((width, rows), BF16),) * count
        + (jax.ShapeDtypeStruct((2 * width, rows), F32),) * count
        + (jax.ShapeDtypeStruct((2 * width, rows), BF16),) * (blocks - count),
        in_specs=[in_smem()] * 2 + [in_vmem()] * (2 * count + blocks + 2),
        out_specs=(in_vmem(),) * (count + blocks),
        scratch_shapes=[
            pltpu.VMEM((count, width, rows), BF16),
            pltpu.VMEM((blocks, group, rows, HEAD_DIM), BF16),
            pltpu.VMEM((blocks, width, rows), BF16),
            pltpu.VMEM((blocks, group, rows, HEAD_DIM), BF16),
            pltpu.VMEM((count, width, rows), BF16),
            pltpu.VMEM((count, 8, rows), F32),
            pltpu.VMEM((count, width, rows), F32),
            pltpu.VMEM((blocks, 2 * width, rows), F32),
        ],
        name="attention_backward",
    )(stretches, length, *queries, *keys, *douts, exact, logsum)
    return outs[:count], outs[count:]


def feed_forward_kernel(hidden_units, parts, place_ref, length_ref, *refs):
    attn_pieces, refs = refs[:parts], refs[parts:]
    (tokens_ref, cotangent_ref, gain_ref), refs = refs[:3], refs[3:]
    others, downs, refs = refs[:4], refs[4:8], refs[8:]
    douts, refs = refs[:parts], refs[parts:]
    (output_ref, d_middle_ref, attn_far_ref, attn_near_ref, d_branch_ref), refs = refs[:5], refs[5:]
    grad_outs, refs = refs[:4], refs[4:]
    out_s, gate_up_s, down_s, d_normed_s, turned_s, middle_s, d_attn_s = refs[:7]
    rows_s, grads_s, sems, grad_sems = refs[7:11], refs[11:15], refs[15], refs[16]
    rows, width = tokens_ref.shape
    core, part, stretch, x_at = place_ref[0], place_ref[1], place_ref[2], place_ref[3]
    quarter = width // 4
    copies = []
    for index, (columns, target, sources) in enumerate(
        (
            (slice(0, width), out_s, others),
            (slice(width, width + 2 * hidden_units), gate_up_s, others),
            (slice(0, hidden_units), down_s, downs),
        )
    ):
        group = []
        for which, source in enumerate(sources):
            x, c = (x_at + which // 2) % 2, (core + which) % 2
            start = pl.multiple_of((2 * x + c) * quarter, 64)
            group.append(
                pltpu.make_async_copy(
                    source.at[:, columns],
                    target.at[pl.ds(start, quarter), :],
                    sems.at[index, which],
                )
            )
        copies.append(group)
    for group in copies:
        for copy in group:
            copy.start()

    def by_core(source, far, near):
        for x in range(2):
            for ref, index in ((far, 1 - core), (near, core)):
                start = pl.multiple_of((2 * x + index) * quarter, 64)
                ref[x * quarter : (x + 1) * quarter, :] = source[pl.ds(start, quarter), :]

    part_width = width // parts
    for shift, piece in enumerate(attn_pieces):
        start = pl.multiple_of((part + shift) % parts * part_width, 64)
        d_attn_s[pl.ds(start, part_width), :] = piece[...]
    by_core(d_attn_s, attn_far_ref, attn_near_ref)
    position = stretch * rows + lax.broadcasted_iota(jnp.int32, (rows, width), 0)
    d_out = jnp.where(position < length_ref[0], cotangent_ref[...].astype(F32), 0.0)
    d_down = (BRANCH_SCALE * d_out).astype(BF16)
    turned_s[...] = jnp.transpose(d_down)
    by_core(turned_s, rows_s[0], rows_s[1])
    attn = jnp.transpose(d_attn_s[...])
    gain = gain_ref[...]
    for copy in copies[0]:
        copy.wait()
    middle = tokens_ref[...].astype(F32) + BRANCH_SCALE * jnp.dot(
        attn, out_s[...], preferred_element_type=F32
    )
    middle_s[...] = middle
    inverse = lax.rsqrt(jnp.mean(middle * middle, axis=-1, keepdims=True) + NORM_EPS)
    normed = (middle * inverse * gain).astype(BF16)
    turned_s[...] = jnp.transpose(normed)
    by_core(turned_s, rows_s[2], rows_s[3])
    d_normed_s[...] = jnp.zeros_like(d_normed_s)
    output_ref[...] = middle
    for copy in copies[1] + copies[2]:
        copy.wait()
    step = 256
    steps = hidden_units // step

    def leaving(index):
        at = pl.ds(pl.multiple_of(index * step, step), step)
        up_at = pl.ds(pl.multiple_of(hidden_units + index * step, step), step)
        for which in range(2):
            for columns in (at,):
                yield pltpu.make_async_copy(
                    grads_s[which].at[:, columns],
                    grad_outs[which].at[:, columns],
                    grad_sems.at[which, index],
                )
            for name, columns in enumerate((at, up_at)):
                yield pltpu.make_async_copy(
                    grads_s[2 + which].at[:, columns],
                    grad_outs[2 + which].at[:, columns],
                    grad_sems.at[2 + 2 * which + name, index],
                )

    def chunk(index, carry):
        at = pl.ds(pl.multiple_of(index * step, step), step)
        up_at = pl.ds(pl.multiple_of(hidden_units + index * step, step), step)
        w_gate, w_up = gate_up_s[:, at], gate_up_s[:, up_at]
        gate = jnp.dot(normed, w_gate, preferred_element_type=F32)
        up = jnp.dot(normed, w_up, preferred_element_type=F32)
        d_hidden = jnp.dot(d_down, down_s[:, at], preferred_element_type=F32)
        sigma = jax.nn.sigmoid(gate)
        silu = gate * sigma
        hidden = (silu * up).astype(BF16)
        d_gate = (d_hidden * up * sigma * (1.0 + gate * (1.0 - sigma))).astype(BF16)
        d_up = (d_hidden * silu).astype(BF16)
        output_ref[...] += BRANCH_SCALE * dot(hidden, down_s[:, at], 1, 1)
        d_normed_s[...] += dot(d_gate, w_gate, 1, 1) + dot(d_up, w_up, 1, 1)
        for which in range(2):
            grads_s[which][:, at] = dot(rows_s[which][...], hidden, 1, 0).astype(BF16)
            grads_s[2 + which][:, at] = dot(rows_s[2 + which][...], d_gate, 1, 0).astype(BF16)
            grads_s[2 + which][:, up_at] = dot(rows_s[2 + which][...], d_up, 1, 0).astype(BF16)
        for copy in leaving(index):
            copy.start()
        return carry

    lax.fori_loop(0, steps, chunk, 0)
    middle = middle_s[...]
    scaled = middle * inverse
    d_scaled = d_normed_s[...] * gain
    d_middle = d_out + norm_back(d_scaled, scaled, inverse)
    d_middle_ref[...] = d_middle
    d_branch = (BRANCH_SCALE * d_middle).astype(BF16)
    d_branch_ref[...] = d_branch
    d_attn_s[...] = dot(out_s[...], d_branch, 1, 1).astype(BF16)
    for shift, dout in enumerate(douts):
        start = pl.multiple_of((part + shift) % parts * part_width, 64)
        dout[...] = d_attn_s[pl.ds(start, part_width), :]

    def left(index, carry):
        for copy in leaving(index):
            copy.wait()
        return carry

    lax.fori_loop(0, steps, left, 0)


def feed_forward(parts, place, length, attn_pieces, tokens, cotangent, gain, others, downs):
    rows, width = tokens.shape
    hidden_units = downs[0].shape[-1]
    shape = jax.ShapeDtypeStruct
    half = shape((width // 2, rows), BF16)
    grads = [(width // 2, hidden_units)] * 2 + [(width // 2, 2 * hidden_units)] * 2
    quarters = (*others, *downs)
    outs = pl.pallas_call(
        functools.partial(feed_forward_kernel, hidden_units, parts),
        out_shape=(shape((width // parts, rows), BF16),) * parts
        + (
            shape((rows, width), F32),
            shape((rows, width), F32),
            half,
            half,
            shape((rows, width), BF16),
        )
        + tuple(shape(grad, BF16) for grad in grads),
        in_specs=[in_smem()] * 2
        + [in_vmem()] * (parts + 3)
        + [pl.BlockSpec(memory_space=pl.ANY)] * 8,
        out_specs=(in_vmem(),) * (parts + 5) + (pl.BlockSpec(memory_space=pl.ANY),) * 4,
        scratch_shapes=[
            pltpu.VMEM((width, width), BF16),
            pltpu.VMEM((width, 2 * hidden_units), BF16),
            pltpu.VMEM((width, hidden_units), BF16),
            pltpu.VMEM((rows, width), F32),
            pltpu.VMEM((width, rows), BF16),
            pltpu.VMEM((rows, width), F32),
            pltpu.VMEM((width, rows), BF16),
        ]
        + [pltpu.VMEM((width // 2, rows), BF16)] * 4
        + [pltpu.VMEM(grad, BF16) for grad in grads]
        + [
            pltpu.SemaphoreType.DMA((3, 4)),
            pltpu.SemaphoreType.DMA((6, hidden_units // 256)),
        ],
        name="feed_forward",
    )(place, length, *attn_pieces, tokens, cotangent, gain.reshape(1, width), *quarters)
    return outs[:parts], outs[parts : parts + 5], outs[parts + 5 :]


def local(
    tokens,
    cotangent,
    lengths,
    stretch_order,
    gain_attn,
    w_query,
    w_key,
    w_value,
    w_out,
    gain_ffn,
    w_gate,
    w_up,
    w_down,
):
    rows, width = tokens.shape
    hidden_units = w_gate.shape[1]
    shard = w_query.shape[0]
    blk_size = lax.axis_size("blk")
    uly_size = lax.axis_size("ulysses")
    dp_size = lax.axis_size("dp")
    assert dp_size == 4 and uly_size == 2
    head_parts = math.gcd(HEADS, blk_size)
    group = HEADS // head_parts
    part_width = group * HEAD_DIM
    members = (blk_size // head_parts) * uly_size
    stretch_count = stretch_order.shape[0]
    assert stretch_count == blk_size * uly_size

    dp_at = lax.axis_index("dp")
    blk_at = lax.axis_index("blk")
    uly_at = lax.axis_index("ulysses")
    x_at, core_at = dp_at // 2, dp_at % 2
    part_at = blk_at % head_parts
    member_at = (blk_at // head_parts) * uly_size + uly_at

    def over_core(value):
        return lax.ppermute(value, "dp", [(i, i ^ 1) for i in range(dp_size)])

    def over_x(value):
        return lax.ppermute(value, "dp", [(i, i ^ 2) for i in range(dp_size)])

    def over_y(value):
        return lax.ppermute(value, "ulysses", [(i, i ^ 1) for i in range(uly_size)])

    def over_blk(value, shift):
        return lax.ppermute(value, "blk", [(i, (i + shift) % blk_size) for i in range(blk_size)])

    def over_part(value, shift):
        return lax.ppermute(
            value,
            "blk",
            [
                (i, i - i % head_parts + (i + shift) % head_parts)
                for i in range(blk_size)
            ],
        )

    def over_member(value, shift):
        pairs = []
        for source in range(blk_size * uly_size):
            blk, uly = divmod(source, uly_size)
            member = (blk // head_parts) * uly_size + uly
            target = (member + shift) % members
            new_blk = (target // uly_size) * head_parts + blk % head_parts
            pairs.append((source, new_blk * uly_size + target % uly_size))
        return lax.ppermute(value, ("blk", "ulysses"), pairs)

    labels = jnp.arange(stretch_count, dtype=jnp.int32)
    places = []
    for member_shift in range(members):
        for part_shift in range(head_parts):
            member = (member_at - member_shift) % members
            part = (part_at - part_shift) % head_parts
            block = (member // uly_size) * head_parts + part
            places.append(block * uly_size + member % uly_size)
    places = jnp.stack(places).astype(jnp.int32)
    stretches = jnp.sum(
        jnp.where(places[:, None] == labels[None, :], stretch_order[None, :], 0), axis=1
    ).astype(jnp.int32)

    own_pos = stretches[0] * rows + jnp.arange(rows, dtype=jnp.int32)
    half_dim = HEAD_DIM // 2
    freqs = jnp.exp(jnp.arange(half_dim, dtype=F32) * (-2.0 * math.log(10000.0) / HEAD_DIM))
    angles = freqs[:, None] * own_pos.astype(F32)[None, :]
    cosine, sine_part = jnp.cos(angles), jnp.sin(angles)

    def rotate(values, direction):
        first = values[..., :half_dim, :]
        second = values[..., half_dim:, :]
        return jnp.concatenate(
            [
                first * cosine - direction * second * sine_part,
                second * cosine + direction * first * sine_part,
            ],
            axis=-2,
        )

    def plane_first(first, second):
        return over_x(first), over_y(second), over_x(second)

    def plane_second(first, second, first_x, second_y, second_x):
        second_xy = over_x(second_y)
        first_y = over_y(first)
        first_xy = over_y(first_x)
        return (first, first_x, first_y, first_xy), (second, second_x, second_y, second_xy)

    def column_pair(mine, by_y):
        here = lax.broadcasted_iota(jnp.int32, (1, 2, 1, 1), 1) == uly_at
        return jnp.where(here, mine[:, None], by_y[:, None]).reshape(width // 4, -1)

    def plane(mine, by_x, by_y, by_xy):
        return in_order(
            x_at, in_order(uly_at, mine, by_y, 1), in_order(uly_at, by_x, by_xy, 1), 0
        )

    def from_line(piece):
        return [piece] + [over_blk(piece, shift) for shift in range(1, blk_size)]

    def line(arrived):
        backwards = jnp.stack([arrived[(-i) % blk_size] for i in range(blk_size)])
        return roll_to(backwards, (blk_size - blk_at) % blk_size)

    def both_cores(half):
        whole = jnp.broadcast_to(half[:, None], half.shape[:1] + (2,) + half.shape[1:])
        start = (0, 1 - core_at) + (0,) * (half.ndim - 1)
        whole = lax.dynamic_update_slice(whole, over_core(half)[:, None], start)
        return whole.reshape(width, -1)

    def by_part(part):
        span = slice(part * part_width, (part + 1) * part_width)
        return [w_key[:, span], w_value[:, span]]

    gains = jnp.pad(jnp.stack([gain_attn, gain_ffn], axis=1), ((0, 0), (0, 126)))
    qkv_local = jnp.concatenate(
        [gains, w_query] + [w for part in range(head_parts) for w in by_part(part)], axis=1
    )
    qkv_line = line(from_line(qkv_local))
    first_columns = 128 + 3 * width // 2
    qkv_halves = lax.optimization_barrier(
        (qkv_line[..., :first_columns], qkv_line[..., first_columns:])
    )
    qkv_firsts = plane_first(*qkv_halves)
    qkv_planes = plane_second(*qkv_halves, *qkv_firsts)
    qkv_half = jnp.concatenate([plane(*pieces) for pieces in qkv_planes], axis=-1)
    qkv_all = both_cores(lax.optimization_barrier(qkv_half))
    gain_attn_all = qkv_all[:, 0].astype(F32)
    gain_ffn_all = qkv_all[:, 1].astype(F32)
    w_qkv = qkv_all[:, 128:]

    rest_local = jnp.concatenate([w_down, w_out, w_gate, w_up], axis=1)
    rest_arrived = from_line(after(rest_local, qkv_halves[0]))

    def pick(values, index, axis):
        return lax.dynamic_index_in_dim(values, index, axis, keepdims=False)

    def by_core(left_t):
        grid = left_t.reshape(2, 2, width // 4, rows)
        return tuple(
            pick(grid, core, 1).reshape(width // 2, rows) for core in (1 - core_at, core_at)
        )

    inputs = tokens.astype(F32)
    scaled_in, inverse_in = normalize(inputs)
    normed_attn = (scaled_in * gain_attn_all[None, :]).astype(BF16)
    qkv_lin = dot(w_qkv, normed_attn, 0, 1)
    q_lin = qkv_lin[:width].reshape(head_parts, group, HEAD_DIM, rows)
    kv_lin = qkv_lin[width:].reshape(head_parts, 2, group, HEAD_DIM, rows)
    q_send = (rotate(q_lin, 1.0).astype(BF16) * SCORE_SCALE).astype(BF16)
    kv_send = jnp.stack(
        [rotate(kv_lin[:, 0], 1.0).astype(BF16), kv_lin[:, 1].astype(BF16)], axis=1
    )

    def scatter_parts(pieces):
        result = []
        for shift in range(head_parts):
            piece = lax.dynamic_index_in_dim(
                pieces, (part_at + shift) % head_parts, 0, keepdims=False
            )
            result.append(over_part(piece, shift) if shift else piece)
        return result

    def send_back(pieces, *earlier):
        return [
            after(over_part(piece, head_parts - shift), *earlier) if shift else piece
            for shift, piece in enumerate(pieces)
        ]

    def return_parts(pieces, *earlier):
        back = jnp.stack(send_back(pieces, *earlier))
        return roll_to(back, (head_parts - part_at) % head_parts)

    keys = scatter_parts(kv_send.reshape(head_parts, 2 * part_width, rows))
    queries = scatter_parts(q_send.reshape(head_parts, part_width, rows))
    keys = keys + [
        over_member(piece, member_shift)
        for member_shift in range(1, members)
        for piece in keys
    ]

    rest_arrived = [after(piece, keys[0]) for piece in rest_arrived]
    rest_line = line(rest_arrived)
    rest_halves = lax.optimization_barrier(
        (rest_line[..., :hidden_units], rest_line[..., hidden_units:])
    )
    rest_firsts = plane_first(*rest_halves)
    other_mine = rest_halves[1][:, None]
    other_mine = jnp.broadcast_to(other_mine, (blk_size, 2) + other_mine.shape[2:])
    other_mine = lax.dynamic_update_slice(
        other_mine, rest_firsts[1][:, None], (0, 1 - uly_at, 0, 0)
    )
    other_mine = lax.optimization_barrier(other_mine.reshape(width // 4, -1))
    other_mine_core = over_core(other_mine)
    rest_planes = plane_second(
        *(after(piece, keys[-1]) for piece in rest_halves),
        *(after(piece, keys[-1]) for piece in rest_firsts),
    )
    (first, first_x, first_y, first_xy), (_, second_x, _, second_xy) = rest_planes
    other_x = lax.optimization_barrier(column_pair(second_x, second_xy))
    down_mine = lax.optimization_barrier(column_pair(first, first_y))
    down_x = lax.optimization_barrier(column_pair(first_x, first_xy))
    others = (other_mine, other_mine_core, other_x, over_core(other_x))
    downs = (down_mine, over_core(down_mine), down_x, over_core(down_x))
    normed_rows, lengths = lax.optimization_barrier(
        (by_core(jnp.transpose(normed_attn)), lengths)
    )
    outs, exact_t, logsum = attention_forward(stretches, lengths, queries, keys, group)
    attn_pieces = send_back(outs)

    d_attns, (output, d_middle, *attn_rows, d_branch), rest_grads = feed_forward(
        head_parts,
        jnp.stack([core_at, part_at, stretches[0], x_at]).astype(jnp.int32),
        lengths,
        attn_pieces,
        tokens,
        cotangent,
        gain_ffn_all,
        others,
        downs,
    )

    douts = [
        over_part(piece, shift) if shift else piece for shift, piece in enumerate(d_attns)
    ]

    def both(mine, theirs):
        return (mine.astype(F32) + theirs.astype(F32)).astype(BF16)

    def core_sum(left_rows, product):
        far = product(left_rows[0]).astype(BF16)
        return core_pair(far, product(left_rows[1]))

    def core_pair(far, near):
        arrived = over_core(far)
        shape = (2, blk_size, 2, shard, -1)
        return near.reshape(shape), arrived.reshape(shape)

    def columns(terms, span):
        return tuple(term[..., span] for term in terms)

    def added(terms, index, axis):
        return sum(pick(term, index, axis).astype(F32) for term in terms).astype(BF16)

    def x_sum(terms, *earlier):
        arrived = over_x(added(terms, 1 - x_at, 0))
        return both(added(terms, x_at, 0), after(arrived, *earlier))

    def y_sum(terms, axis, *earlier):
        arrived = over_y(added(terms, 1 - uly_at, axis))
        return both(added(terms, uly_at, axis), after(arrived, *earlier))

    def line_sum(values, *earlier):
        total = pick(values, blk_at, 0).astype(F32)
        for shift in range(1, blk_size):
            piece = pick(values, (blk_at + shift) % blk_size, 0)
            total = total + after(over_blk(piece, shift), *earlier).astype(F32)
        return total

    down_sum_core = core_pair(rest_grads[0], rest_grads[1])
    gate_up_core = core_pair(rest_grads[2], rest_grads[3])
    out_core = core_sum(attn_rows, lambda l: dot(l, d_branch, 1, 0))

    dq, dkv = attention_backward(stretches, lengths, queries, keys, douts, exact_t, logsum, group)
    d_q = return_parts(dq).reshape(HEADS, HEAD_DIM, rows)
    d_q_t = rotate(d_q.astype(F32), -1.0).astype(BF16).reshape(width, rows)
    q_core = core_sum(normed_rows, lambda l: dot(l, d_q_t, 1, 1))
    back = []
    for shift in range(head_parts):
        total = dkv[shift]
        for member_shift in range(1, members):
            theirs = dkv[member_shift * head_parts + shift]
            total = total + over_member(theirs, members - member_shift).astype(F32)
        back.append(total.astype(BF16))
    d_kv = return_parts(back, *q_core)
    q_x = x_sum(q_core)
    gate_x = x_sum(columns(gate_up_core, slice(0, hidden_units)), back[-1])
    up_y = y_sum(columns(gate_up_core, slice(hidden_units, None)), 2, dkv[0])
    gate_sum = y_sum((gate_x,), 1, d_kv)
    up_sum = x_sum((up_y,), back[-1])
    down_y = y_sum(down_sum_core, 2, dkv[0])
    down_sum = x_sum((down_y,), back[-1])
    out_sum = y_sum((x_sum(out_core, back[-1]),), 1, d_kv)
    d_kv = d_kv.reshape(head_parts, 2, group, HEAD_DIM, rows)
    d_kv_t = jnp.stack(
        [rotate(d_kv[:, 0].astype(F32), -1.0).astype(BF16), d_kv[:, 1]], axis=1
    ).reshape(2 * width, rows)

    kv_core = core_sum(normed_rows, lambda l: dot(l, d_kv_t, 1, 1))
    k_x = x_sum(columns(kv_core, slice(0, width)))
    v_y = y_sum(columns(kv_core, slice(width, None)), 2)
    q_sum = y_sum((q_x,), 1)
    k_sum = y_sum((k_x,), 1)
    v_sum = x_sum((v_y,))

    rest_sum = line_sum(jnp.concatenate([down_sum, out_sum, gate_sum, up_sum], axis=-1), q_sum, k_sum, v_sum)
    qkv_sum = line_sum(jnp.concatenate([q_sum, k_sum, v_sum], axis=-1))

    d_normed = dot(d_q_t, w_qkv[:, :width], 0, 1) + dot(d_kv_t, w_qkv[:, width:], 0, 1)
    d_inputs = d_middle + norm_back(d_normed * gain_attn_all[None, :], scaled_in, inverse_in)

    grad_query = qkv_sum[:, :width]
    grad_kv = qkv_sum[:, width:].reshape(shard, head_parts, 2, part_width)
    grad_key = grad_kv[:, :, 0].reshape(shard, width)
    grad_value = grad_kv[:, :, 1].reshape(shard, width)
    grad_down = rest_sum[:, :hidden_units]
    grad_out = rest_sum[:, hidden_units : hidden_units + width]
    grad_gate = rest_sum[:, hidden_units + width : 2 * hidden_units + width]
    grad_up = rest_sum[:, 2 * hidden_units + width :]

    def gain_grad(gain, pairs):
        total = sum(jnp.sum(w.astype(F32) * grad, axis=1) for w, grad in pairs)
        return total / gain.astype(F32)

    return (
        output,
        d_inputs,
        gain_grad(gain_attn, [(w_query, grad_query), (w_key, grad_key), (w_value, grad_value)]),
        grad_query,
        grad_key,
        grad_value,
        grad_out,
        gain_grad(gain_ffn, [(w_gate, grad_gate), (w_up, grad_up)]),
        grad_gate,
        grad_up,
        grad_down,
    )


def solution(mesh):
    row, flat = P(ALL, None), P(ALL)
    in_specs = (row, row, P("dp"), P(), flat, row, row, row, row, flat, row, row, row)
    out_specs = (row, row, flat, row, row, row, row, flat, row, row, row)
    return jax.shard_map(local, mesh=mesh, in_specs=in_specs, out_specs=out_specs, check_vma=False)
```
